256 devices in a mesh: blk: 128 (over y, z, x), rep: 2 (over core).
Axes of the slice: x: 4, y: 4, z: 8, core: 2. Of those that a mesh axis runs over, the one named last changes fastest.
Arguments:
- features: bfloat16 [32768, 256], P('blk', 'rep'), may hold values from -6 to 6
- observations: bfloat16 [256, 128], P('blk'), may hold values from -6 to 6
- cond_ids: int32 [256, 4], P('blk'), may hold values from 0 to 255, as said below
Outputs:
- block_loglik: float32 [256], P(('blk', 'rep'))
- feature_grad: float32 [32768, 256], P('blk', 'rep')
The draws below stay inside these ranges and needn't reach their ends.
Inputs may be any that keep to these rules, and one draw needn't show every extreme that they name: `cond_ids`: row b names 4 different blocks, none of them b. Entry 0 is block (b - 1) mod 256; entry 1 is block (b - a) mod 256 for some a from 2 to 4; the remaining entries of all rows together name exactly 8 distinct blocks.
All inputs are finite; a program needn't handle non-finite values.
Results may differ from the reference program's by a relative error of at most 0.017.
Values may be sent and summed in bfloat16 or wider, within the bound.
A program may use at most 64 MiB of HBM per device.

```python
import math
import jax
import jax.numpy as jnp
from jax import lax

P_SIZE = 128
F = 256
NCOND = 4
HOT = 8
BLK_DEV = 2
NBLK = 256
POINTS = 32768


def draw_features(key, part):
    key_c, key_g, key_n = jax.random.split(key, 3)
    groups = jax.random.randint(key_g, (POINTS,), 0, 64, dtype=jnp.int32)
    centers = jax.random.normal(key_c, (64, F), jnp.float32)
    noise = jax.random.normal(key_n, (POINTS, F), jnp.float32)
    values = 1.1 * centers[groups] + 0.6 * noise
    return jnp.clip(values, -6.0, 6.0).astype(jnp.bfloat16)


def draw_cond_ids(key, part):
    key_a, key_b, key_c = jax.random.split(key, 3)
    blocks = jnp.arange(NBLK, dtype=jnp.int32)
    first = (blocks - 1) % NBLK
    offset = jax.random.randint(key_a, (NBLK,), 2, 2 * BLK_DEV + 1, dtype=jnp.int32)
    second = (blocks - offset) % NBLK
    hot = jax.random.permutation(key_b, NBLK)[:HOT].astype(jnp.int32)
    clash = (hot[None, :] == first[:, None]) | (hot[None, :] == second[:, None]) | (hot[None, :] == blocks[:, None])
    scores = jax.random.randint(key_c, (NBLK, HOT), 0, 1 << 16, dtype=jnp.int32) * HOT
    scores = scores + jnp.arange(HOT, dtype=jnp.int32)[None, :] - clash.astype(jnp.int32) * (1 << 24)
    unused, picked = lax.top_k(scores, NCOND - 2)
    far = hot[picked]
    return jnp.concatenate([first[:, None], second[:, None], far], axis=1)


def levels(rng, extent, cuts, smallest, high):
    def one(axis_at, blocks):
        heights = jax.random.uniform(jax.random.fold_in(jax.random.fold_in(rng, 6), axis_at), (blocks,), jnp.float32, smallest / len(cuts), high / len(cuts))
        return jnp.repeat(jnp.exp(heights), extent[axis_at] // blocks).reshape((-1,) + (1,) * (len(extent) - axis_at - 1))

    gain = one(*cuts[0])
    for cut in cuts[1:]:
        gain = gain * one(*cut)
    return gain


def centred(own_key, shape, scale, limit, cuts=(), kind=jnp.bfloat16):
    factor_of = levels(own_key, shape, cuts, -0.22, 0.18) if cuts else 1.0
    values = jax.random.normal(own_key, shape, jnp.float32) * scale * factor_of
    return jnp.minimum(jnp.maximum(values, -limit), limit).astype(kind)


def setup_inputs(seed: int = 0) -> dict:
    seeds = jax.random.split(jax.random.key(seed), 4)
    return {
        "features": draw_features(jax.random.fold_in(seeds[3], 71), 0),
        "observations": centred(seeds[1], (NBLK, P_SIZE), 1.0, 6.0, ((0, 128),)),
        "cond_ids": draw_cond_ids(jax.random.fold_in(seeds[3], 71), 0),
    }


def block_terms(joint_x, joint_y, own):
    joint = joint_x.shape[0]
    width = joint_x.shape[1]
    wide_x = joint_x.astype(jnp.float32)
    squares = lax.optimization_barrier(jnp.sum(wide_x * wide_x, axis=1))
    gram = jnp.dot(joint_x.astype(jnp.float32), joint_x.T.astype(jnp.float32), preferred_element_type=jnp.float32)
    dist = squares[:, None] + squares[None, :] - 2.0 * gram
    diag_mask = jnp.eye(joint, dtype=bool)
    ident = jnp.eye(joint, dtype=jnp.float32)

    def loglik_of(dist_in):
        kern = jnp.where(diag_mask, 1.0, jnp.exp(-dist_in * (0.5 / width)))
        sigma = kern + 0.1 * ident
        chol = jnp.linalg.cholesky(sigma)
        solved = jax.scipy.linalg.solve_triangular(chol, joint_y, lower=True)
        tail = solved[joint - own:]
        logs = jnp.log(jnp.diagonal(chol)[joint - own:])
        return -0.5 * jnp.sum(tail * tail) - jnp.sum(logs) - 0.5 * own * math.log(2.0 * math.pi)
    value, pull = jax.vjp(loglik_of, dist)
    weight = pull(jnp.ones((), dist.dtype))[0]
    sym = (weight + weight.T).astype(jnp.bfloat16)
    rowsum = lax.optimization_barrier(jnp.sum(sym.astype(jnp.float32), axis=1))
    grad = 2.0 * (rowsum[:, None] * wide_x - jnp.dot(sym.astype(jnp.float32), joint_x.astype(jnp.float32), preferred_element_type=jnp.float32))
    return (value, grad)

def reference(features, observations, cond_ids):
    width = features.shape[1]
    blocks = features.reshape(NBLK, P_SIZE, width)
    obs = observations.astype(jnp.float32)
    slots = jnp.concatenate([cond_ids, jnp.arange(NBLK, dtype=jnp.int32)[:, None]], axis=1)

    def step(total, index):
        chosen = slots[index]
        joint_x = blocks[chosen].reshape(-1, width)
        joint_y = obs[chosen].reshape(-1)
        value, grad = block_terms(joint_x, joint_y, P_SIZE)
        total = total.at[chosen].add(grad.reshape(NCOND + 1, P_SIZE, width))
        return (total, value)
    start = jnp.zeros((NBLK, P_SIZE, width), jnp.float32)
    total, values = lax.scan(step, start, jnp.arange(NBLK, dtype=jnp.int32))
    return (values, total.reshape(NBLK * P_SIZE, width))
```

```python
import functools
import math

import jax
import jax.numpy as jnp
from jax import lax
from jax.experimental import pallas as pl
from jax.experimental.pallas import tpu as pltpu
from jax.sharding import PartitionSpec as P

HOT = 8
T = 128
G = 8
VMEM = pl.BlockSpec(memory_space=pltpu.VMEM)
HI = lax.Precision.HIGHEST


def dot32(a, b, dims=((1,), (0,))):
    return lax.dot_general(a, b, (dims, ((), ())), precision=HI, preferred_element_type=jnp.float32)


def negative_inverse(ref):
    lane = lax.broadcasted_iota(jnp.int32, (G, T), 1)
    sub = lax.broadcasted_iota(jnp.int32, (G, T), 0)

    def group(step, logs):
        a = ref[...]
        cols = [jnp.broadcast_to(a[:, k : k + 1], (T, T)) for k in range(G)]
        rows = []
        for k in range(G):
            row = jnp.broadcast_to(a[k : k + 1, :], (G, T))
            rows.append(jnp.where(lane < G, jnp.where(lane == k, -1.0, 0.0), row))
        s = {}
        for k in range(G):
            for i in range(k, G):
                s[i, k] = jnp.broadcast_to(cols[k][i : i + 1, :], (G, T))
        inv = []
        low = {}
        prod = None
        for k in range(G):
            d = s[k, k]
            prod = d if prod is None else prod * d
            r = 1.0 / d
            inv.append(r)
            for i in range(k + 1, G):
                low[i, k] = s[i, k] * r
            for i in range(k + 1, G):
                for m in range(k + 1, i + 1):
                    s[i, m] = s[i, m] - low[i, k] * s[m, k]
                rows[i] = rows[i] - low[i, k] * rows[k]
        for k in reversed(range(G)):
            x = rows[k] * inv[k]
            for i in range(k + 1, G):
                x = x - low[i, k] * rows[i]
            rows[k] = x
        top = rows[0]
        for k in range(1, G):
            top = jnp.where(sub == k, rows[k], top)
        for t in range(1, T // G):
            blk = jnp.where(lane < G, 0.0, a[t * G : (t + 1) * G, :])
            for k in range(G):
                blk = blk - cols[k][t * G : (t + 1) * G, :] * rows[k]
            ref[(t - 1) * G : t * G, :] = pltpu.roll(blk, T - G, 1)
        ref[T - G :, :] = pltpu.roll(top, T - G, 1)
        return logs + jnp.log(prod)

    return lax.fori_loop(0, T // G, group, jnp.zeros((G, T), jnp.float32))


def block_kernel(nb, slot_ref, mine_ref, other_ref, value_ref, gmine_ref, gother_ref, x_ref, kern, work, piv, right, ext):
    joint, width = x_ref.shape
    lead = joint - T
    for k in range(nb):
        rs = pl.ds(k * T, T)
        x_ref[rs, :T] = mine_ref[slot_ref[k], :T, :]
        x_ref[rs, T:] = other_ref[slot_ref[k], :T, :]
        obs = mine_ref[slot_ref[k], T:, :].astype(jnp.float32)[0:1, :]
        work[rs, joint:] = jnp.transpose(jnp.broadcast_to(obs, (T, T)))
    wide = x_ref[...].astype(jnp.float32)
    sq = jnp.sum(wide * wide, axis=1, keepdims=True)
    sq_row = jnp.transpose(jnp.broadcast_to(sq, (joint, T)))[0:1, :]
    col = lax.broadcasted_iota(jnp.int32, (T, joint), 1)
    row = lax.broadcasted_iota(jnp.int32, (T, joint), 0)
    for k in range(nb):
        rs = pl.ds(k * T, T)
        gram = lax.dot_general(
            x_ref[rs, :], x_ref[...], (((1,), (1,)), ((), ())), preferred_element_type=jnp.float32
        )
        dist = sq[k * T : (k + 1) * T] + sq_row - 2.0 * gram
        kr = jnp.where(col == row + k * T, 1.1, jnp.exp(-dist * (0.5 / width)))
        kern[rs, :] = kr
        work[rs, :joint] = kr
    for k in range(nb - 1):
        a, b = k * T, (k + 1) * T
        piv[...] = work[a:b, a:b]
        negative_inverse(piv)
        t = -dot32(piv[...], work[a:b, b:])
        work[b:, b:] = work[b:, b:] - dot32(work[b:, a:b], t)
        work[a:b, b:] = t
    right[lead - T :, :] = work[lead - T : lead, lead:]
    for k in reversed(range(nb - 2)):
        a, b = k * T, (k + 1) * T
        right[a:b, :] = work[a:b, lead:] - dot32(work[a:b, b:lead], right[b:, :])
    piv[...] = work[lead:, lead:joint]
    res = work[lead:, joint:]
    logs = negative_inverse(piv)
    sinv = -piv[...]
    u = dot32(sinv, res)
    quad = jnp.sum(res * u, axis=0, keepdims=True)
    value_ref[...] = -0.5 * (quad + logs) - 0.5 * T * math.log(2.0 * math.pi)
    inner = sinv - u * jnp.transpose(u)
    ident = jnp.where(
        lax.broadcasted_iota(jnp.int32, (T, T), 0) == lax.broadcasted_iota(jnp.int32, (T, T), 1), 1.0, 0.0
    )
    lane = lax.broadcasted_iota(jnp.int32, (T, T), 1)
    for k in range(nb):
        rs = slice(k * T, (k + 1) * T)
        e = -right[rs, :T] if k < nb - 1 else ident
        alpha = right[rs, T:] if k < nb - 1 else jnp.zeros((T, T), jnp.float32)
        v = dot32(e, u)
        ext[rs, :T] = e
        ext[rs, T:] = jnp.where(lane == 0, v, jnp.where(lane == 1, alpha, 0.0))
        work[rs, :T] = -dot32(e, inner)
        work[rs, T : 2 * T] = jnp.where(lane == 0, alpha, jnp.where(lane == 1, v, 0.0))
    gmine_ref[...] = jnp.zeros_like(gmine_ref)
    gother_ref[...] = jnp.zeros_like(gother_ref)
    for k in range(nb):
        rs = slice(k * T, (k + 1) * T)
        m = dot32(work[rs, : 2 * T], ext[...], ((1,), (1,)))
        sym = jnp.where(col == row + k * T, 0.0, m * kern[rs, :] * (-0.5 / width)).astype(jnp.bfloat16)
        rowsum = jnp.sum(sym.astype(jnp.float32), axis=1, keepdims=True)
        part = jnp.dot(sym, x_ref[...], preferred_element_type=jnp.float32)
        grad = 2.0 * (rowsum * x_ref[rs, :].astype(jnp.float32) - part)
        gmine_ref[slot_ref[k]] = grad[:, :T].astype(jnp.bfloat16)
        gother_ref[slot_ref[k]] = grad[:, T:].astype(jnp.bfloat16)


NX, NZ, NY = 4, 8, 4
NEAR = 2
OWN = 2
PACK = T + 16
NPOOL = OWN * (NEAR + 1) + HOT
MESH = pl.DeviceIdType.MESH


class Place:
    def __init__(self):
        self.blk = lax.axis_index("blk")
        self.rep = lax.axis_index("rep")
        self.x = self.blk % NX
        self.z = self.blk // NX % NZ
        self.y = self.blk // (NX * NZ)

    def along_x(self, by):
        return self.blk - self.x + (self.x + by) % NX, self.rep

    def along_z(self, by):
        return self.blk + ((self.z + by) % NZ - self.z) * NX, self.rep

    def along_y(self, by):
        return (self.blk + by * NX * NZ) % (NX * NZ * NY), self.rep

    def along_blk(self, by):
        return (self.blk + by) % (NX * NZ * NY), self.rep

    def partner(self):
        return self.blk, 1 - self.rep

    def greet(self):
        there = [self.along_z(o) for o in range(1, NZ)]
        there += [self.along_x(o) for o in range(1, NX)]
        there += [self.along_y(o) for o in range(1, NY)]
        there += [self.along_blk(o) for o in (1, 2, -1, -2)]
        there += [self.partner()]
        barrier = pltpu.get_barrier_semaphore()
        for device in there:
            pl.semaphore_signal(barrier, inc=1, device_id=device, device_id_type=MESH)
        pl.semaphore_wait(barrier, len(there))


def send(src, dst, sems, index, device):
    copy = pltpu.make_async_remote_copy(
        src_ref=src,
        dst_ref=dst,
        send_sem=sems.at[0, index],
        recv_sem=sems.at[1, index],
        device_id=device,
        device_id_type=MESH,
    )
    copy.start()
    return copy


def share(src, got, sems, where, count):
    copies = [send(src, got.at[o - 1], sems, o - 1, where(o)) for o in range(1, count)]
    for copy in copies:
        copy.wait()
    total = src[...].astype(jnp.float32)
    for o in range(1, count):
        total = total + got[o - 1].astype(jnp.float32)
    return total


def sum_slots(place, slots, result, zgot, xgot, ygot, held, zs, xs, ys, gs):
    z = place.z
    copies = []
    for o in range(1, NZ):
        copies.append(send(slots.at[(z + o) % NZ], zgot.at[o - 1], zs, o - 1, place.along_z(o)))
    for copy in copies:
        copy.wait()
    total = slots[z].astype(jnp.float32)
    for o in range(1, NZ):
        total = total + zgot[o - 1].astype(jnp.float32)
    held[0] = total.astype(held.dtype)
    total = share(held.at[0], xgot, xs, place.along_x, NX)
    held[1] = total.astype(held.dtype)
    total = share(held.at[1], ygot, ys, place.along_y, NY)
    held[2] = total.astype(held.dtype)
    copies = [send(held.at[2], result.at[z], gs, o - 1, place.along_z(o)) for o in range(1, NZ)]
    result[z] = held[2]
    for copy in copies:
        copy.wait()


def pick_weights(place, marks):
    ids = lax.broadcasted_iota(jnp.int32, (G, T), 0) * T + lax.broadcasted_iota(jnp.int32, (G, T), 1)
    named = jnp.where(marks > 0.5, 1.0, 0.0)
    weights = []
    for c in range(OWN):
        own = place.blk * OWN + c
        here = jnp.sum(jnp.where(ids == own, named, 0.0), keepdims=True)
        rank = jnp.sum(jnp.where(ids < own, named, 0.0), keepdims=True)
        weights.append([here * jnp.where(jnp.abs(rank - s) < 0.5, 1.0, 0.0) for s in range(HOT)])
    return weights


def gather_kernel(cond_ref, own_ref, pool_ref, other_ref, marks_ref, m0, m1, m2, mz, mx, my,
                  slots, hot, zgot, xgot, ygot, held, ms, ns, zs, xs, ys, gs, ps):
    place = Place()
    place.greet()
    near = []
    for by in (1, 2):
        near.append(send(own_ref, pool_ref.at[pl.ds(by * OWN, OWN)], ns, by - 1, place.along_blk(by)))
    ids = lax.broadcasted_iota(jnp.int32, (G, T), 0) * T + lax.broadcasted_iota(jnp.int32, (G, T), 1)
    marks = jnp.zeros((G, T), jnp.float32)
    for c in range(OWN):
        for k in (2, 3):
            marks = jnp.where(ids == cond_ref[c, k], 1.0, marks)
    m0[...] = marks
    pool_ref[:OWN] = own_ref[...]
    m1[...] = share(m0, mz, ms.at[:, pl.ds(0, NZ - 1)], place.along_z, NZ)
    m2[...] = share(m1, mx, ms.at[:, pl.ds(NZ - 1, NX - 1)], place.along_x, NX)
    marks = share(m2, my, ms.at[:, pl.ds(NZ + NX - 2, NY - 1)], place.along_y, NY)
    marks_ref[...] = marks
    weights = pick_weights(place, marks)
    for s in range(HOT):
        value = weights[0][s] * own_ref[0].astype(jnp.float32)
        for c in range(1, OWN):
            value = value + weights[c][s] * own_ref[c].astype(jnp.float32)
        slots[s] = value.astype(jnp.bfloat16)
    early = [send(own_ref, other_ref.at[pl.ds(0, OWN)], ps, 0, place.partner())]
    for by in (1, 2):
        near[by - 1].wait()
        part = pl.ds(by * OWN, OWN)
        early.append(send(pool_ref.at[part], other_ref.at[part], ps, by, place.partner()))
    sum_slots(place, slots, hot, zgot, xgot, ygot, held, zs, xs, ys, gs)
    part = pl.ds(OWN * (NEAR + 1), HOT)
    early.append(send(hot, other_ref.at[part], ps, NEAR + 1, place.partner()))
    pool_ref[part] = hot[...]
    for copy in early:
        copy.wait()


def return_kernel(marks_ref, mine_ref, theirs_ref, out_ref, got, near_out, near_got,
                  slots, hot, zgot, xgot, ygot, held, ns, zs, xs, ys, gs, ps):
    place = Place()
    place.greet()
    parts = [pl.ds(OWN * (NEAR + 1), HOT), pl.ds(0, OWN * (NEAR + 1))]
    copies = [send(theirs_ref.at[p], got.at[p], ps, i, place.partner()) for i, p in enumerate(parts)]
    copies[0].wait()
    part = parts[0]
    slots[...] = (mine_ref[part].astype(jnp.float32) + got[part].astype(jnp.float32)).astype(jnp.bfloat16)
    copies[1].wait()
    part = pl.ds(OWN, OWN * NEAR)
    near_out[...] = (mine_ref[part].astype(jnp.float32) + got[part].astype(jnp.float32)).astype(jnp.bfloat16)
    near = []
    for by in (1, 2):
        part = pl.ds((by - 1) * OWN, OWN)
        near.append(send(near_out.at[part], near_got.at[part], ns, by - 1, place.along_blk(-by)))
    sum_slots(place, slots, hot, zgot, xgot, ygot, held, zs, xs, ys, gs)
    weights = pick_weights(place, marks_ref[...])
    for copy in near:
        copy.wait()
    for c in range(OWN):
        total = mine_ref[c].astype(jnp.float32) + got[c].astype(jnp.float32)
        for by in range(NEAR):
            total = total + near_got[by * OWN + c].astype(jnp.float32)
        for s in range(HOT):
            total = total + weights[c][s] * hot[s].astype(jnp.float32)
        out_ref[c * T : (c + 1) * T, :] = total


def ring_scratch(rows):
    half = jnp.bfloat16
    return [
        pltpu.VMEM((HOT, rows, T), half),
        pltpu.VMEM((HOT, rows, T), half),
        pltpu.VMEM((NZ - 1, rows, T), half),
        pltpu.VMEM((NX - 1, rows, T), half),
        pltpu.VMEM((NY - 1, rows, T), half),
        pltpu.VMEM((3, rows, T), half),
    ]


def dma(count):
    return pltpu.SemaphoreType.DMA((2, count))


def ring_sems():
    return [dma(NEAR), dma(NZ - 1), dma(NX - 1), dma(NY - 1), dma(NZ - 1)]


def body(features, observations, cond_ids):
    per_dev = cond_ids.shape[0]
    ncond = cond_ids.shape[1]
    half = features.shape[1]
    joint = (ncond + 1) * T
    device = lax.axis_index("blk")
    core = lax.axis_index("rep")
    obs = jnp.broadcast_to(observations[:, None, :], (per_dev, PACK - T, T))
    own = jnp.concatenate([features.reshape(per_dev, T, half), obs], axis=1)
    small = pltpu.VMEM((G, T), jnp.float32)
    pool, other, marks = pl.pallas_call(
        gather_kernel,
        out_shape=(
            jax.ShapeDtypeStruct((NPOOL, PACK, T), jnp.bfloat16),
            jax.ShapeDtypeStruct((NPOOL, PACK, T), jnp.bfloat16),
            jax.ShapeDtypeStruct((G, T), jnp.float32),
        ),
        in_specs=[pl.BlockSpec(memory_space=pltpu.SMEM), VMEM],
        out_specs=(VMEM, VMEM, VMEM),
        scratch_shapes=[small] * 3
        + [pltpu.VMEM((n - 1, G, T), jnp.float32) for n in (NZ, NX, NY)]
        + ring_scratch(PACK)
        + [dma(NZ + NX + NY - 3)]
        + ring_sems()
        + [dma(NEAR + 2)],
        compiler_params=pltpu.CompilerParams(
            collective_id=0, has_side_effects=True, vmem_limit_bytes=30 << 20
        ),
        name="gather_blocks",
    )(cond_ids, own)
    named = (marks[:2].reshape(-1) > 0.5).astype(jnp.int32)
    mine = lax.dynamic_index_in_dim(cond_ids, core, 0, keepdims=False)
    near_ids = mine[:2]
    near_slots = (device - near_ids // OWN) % (NX * NZ * NY) * OWN + near_ids % OWN
    below = jnp.arange(named.shape[0], dtype=jnp.int32)[None, :] < mine[2:, None]
    hot_slots = OWN * (NEAR + 1) + jnp.sum(jnp.where(below, named[None, :], 0), axis=1)
    slots = jnp.concatenate([near_slots, hot_slots, core[None].astype(jnp.int32)])
    value, gmine, gother = pl.pallas_call(
        functools.partial(block_kernel, ncond + 1),
        out_shape=(
            jax.ShapeDtypeStruct((G, T), jnp.float32),
            jax.ShapeDtypeStruct((NPOOL, T, T), jnp.bfloat16),
            jax.ShapeDtypeStruct((NPOOL, T, T), jnp.bfloat16),
        ),
        in_specs=[pl.BlockSpec(memory_space=pltpu.SMEM), VMEM, VMEM],
        out_specs=(VMEM, VMEM, VMEM),
        scratch_shapes=[
            pltpu.VMEM((joint, 2 * T), jnp.bfloat16),
            pltpu.VMEM((joint, joint), jnp.float32),
            pltpu.VMEM((joint, joint + T), jnp.float32),
            pltpu.VMEM((T, T), jnp.float32),
            pltpu.VMEM((joint - T, 2 * T), jnp.float32),
            pltpu.VMEM((joint, 2 * T), jnp.float32),
        ],
        compiler_params=pltpu.CompilerParams(vmem_limit_bytes=40 << 20),
        name="block_terms",
    )(slots, pool, other)
    grad = pl.pallas_call(
        return_kernel,
        out_shape=jax.ShapeDtypeStruct((per_dev * T, half), jnp.float32),
        in_specs=[VMEM] * 3,
        out_specs=VMEM,
        scratch_shapes=[
            pltpu.VMEM((NPOOL, T, T), jnp.bfloat16),
            pltpu.VMEM((OWN * NEAR, T, T), jnp.bfloat16),
            pltpu.VMEM((OWN * NEAR, T, T), jnp.bfloat16),
        ]
        + ring_scratch(T)
        + ring_sems()
        + [dma(2)],
        compiler_params=pltpu.CompilerParams(
            collective_id=1, has_side_effects=True, vmem_limit_bytes=30 << 20
        ),
        name="return_gradients",
    )(marks, gmine, gother)
    return (value[0, :1], grad)


def solution(mesh):
    placed = (P("blk", "rep"), P("blk", None), P("blk", None))
    return jax.shard_map(
        body,
        mesh=mesh,
        in_specs=placed,
        out_specs=(P(("blk", "rep")), P("blk", "rep")),
        check_vma=False,
    )
```

```python
import math

import jax
import jax.numpy as jnp
from jax import lax
from jax.experimental import pallas as pl
from jax.experimental.pallas import tpu as pltpu
from jax.sharding import PartitionSpec as P

HOT = 8
T = 128
G = 8
VMEM = pl.BlockSpec(memory_space=pltpu.VMEM)
HI = lax.Precision.HIGHEST


def dot32(a, b, dims=((1,), (0,))):
    return lax.dot_general(a, b, (dims, ((), ())), precision=HI, preferred_element_type=jnp.float32)


UNROLL = 8


def add_up(terms):
    while len(terms) > 1:
        odd = terms[-1:] if len(terms) % 2 else []
        terms = [a + b for a, b in zip(terms[::2], terms[1::2])] + odd
    return terms[0]


def invert_rows(rows, s):
    prod = None
    inv = {}
    for k in range(0, G, 2):
        j = k + 1
        a, b, c = s[k, k], s[j, k], s[j, j]
        det = a * c - b * b
        prod = det if prod is None else prod * det
        r = 1.0 / det
        ra, rb, rc = a * r, b * r, c * r
        inv[k] = (ra, rb, rc)
        rest = [i for i in range(G) if i not in (k, j)]
        low = {}
        for m in range(j + 1, G):
            s[k, m], s[j, m] = s[m, k], s[m, j]
        for i in rest:
            p, q = s[i, k], s[i, j]
            low[i] = (p * rc - q * rb, q * ra - p * rb)
        for i in rest:
            for m in range(j + 1, G):
                if i < k or i >= m:
                    sk, sj = s[m, k], s[m, j]
                    s[i, m] = s[i, m] - (low[i][0] * sk + low[i][1] * sj)
        for i in rest:
            rows[i] = rows[i] - (low[i][0] * rows[k] + low[i][1] * rows[j])
    for k in range(0, G, 2):
        ra, rb, rc = inv[k]
        x, y = rows[k], rows[k + 1]
        rows[k], rows[k + 1] = rc * x - rb * y, ra * y - rb * x
    return prod


def negative_inverse(ref):
    lane = lax.broadcasted_iota(jnp.int32, (G, T), 1)
    sub = lax.broadcasted_iota(jnp.int32, (G, T), 0)
    count = T // G

    def groups(step, logs):
        blks = [ref[t * G : (t + 1) * G, :] for t in range(count)]
        for u in range(UNROLL):
            first = u * G
            inside = (lane >= first) & (lane < first + G)
            panel = blks[u]
            rows = []
            for k in range(G):
                row = jnp.broadcast_to(panel[k : k + 1, :], (G, T))
                rows.append(jnp.where(inside, jnp.where(lane == first + k, -1.0, 0.0), row))
            s = {}
            for k in range(G):
                col = jnp.broadcast_to(panel[:, first + k : first + k + 1], (G, T))
                for i in range(k, G):
                    s[i, k] = jnp.broadcast_to(col[i : i + 1, :], (G, T))
                    s[k, i] = s[i, k]
            prod = invert_rows(rows, s)
            logs = logs + jnp.log(prod)
            order = [(u + d) % count for d in range(1, count)]
            for t in order:
                old = blks[t]
                terms = [
                    jnp.broadcast_to(old[:, first + k : first + k + 1], (G, T)) * rows[k] for k in range(G)
                ]
                blks[t] = jnp.where(inside, 0.0, old) - add_up(terms)
            top = rows[0]
            for k in range(1, G):
                top = jnp.where(sub == k, rows[k], top)
            blks[u] = top
        shift = UNROLL * G
        for t in range(count):
            at = (t - UNROLL) % count
            ref[at * G : (at + 1) * G, :] = blks[t] if shift == T else pltpu.roll(blks[t], T - shift, 1)
        return logs

    zero = jnp.zeros((G, T), jnp.float32)
    if UNROLL == count:
        return groups(0, zero)
    return lax.fori_loop(0, count // UNROLL, groups, zero)


NX, NZ, NY = 4, 8, 4
NEAR = 2
OWN = 2
PACK = T + 16
MESH = pl.DeviceIdType.MESH


class Place:
    def __init__(self):
        self.blk = lax.axis_index("blk")
        self.rep = lax.axis_index("rep")
        self.x = self.blk % NX
        self.z = self.blk // NX % NZ
        self.y = self.blk // (NX * NZ)

    def along_x(self, by):
        return self.blk - self.x + (self.x + by) % NX, self.rep

    def along_z(self, by):
        return self.blk + ((self.z + by) % NZ - self.z) * NX, self.rep

    def along_y(self, by):
        return (self.blk + by * NX * NZ) % (NX * NZ * NY), self.rep

    def along_blk(self, by):
        return (self.blk + by) % (NX * NZ * NY), self.rep

    def partner(self):
        return self.blk, 1 - self.rep

    def greet(self):
        there = [self.along_z(o) for o in range(1, NZ)]
        there += [self.along_x(o) for o in range(1, NX)]
        there += [self.along_y(o) for o in range(1, NY)]
        there += [self.along_blk(o) for o in (1, 2, -1, -2)]
        there += [self.partner()]
        barrier = pltpu.get_barrier_semaphore()
        for device in there:
            pl.semaphore_signal(barrier, inc=1, device_id=device, device_id_type=MESH)
        pl.semaphore_wait(barrier, len(there))


def send(src, dst, sems, index, device):
    copy = pltpu.make_async_remote_copy(
        src_ref=src,
        dst_ref=dst,
        send_sem=sems.at[0, index],
        recv_sem=sems.at[1, index],
        device_id=device,
        device_id_type=MESH,
    )
    copy.start()
    return copy


def pick_weights(place, marks):
    ids = lax.broadcasted_iota(jnp.int32, (G, T), 0) * T + lax.broadcasted_iota(jnp.int32, (G, T), 1)
    named = jnp.where(marks > 0.5, 1.0, 0.0)
    weights = []
    for c in range(OWN):
        own = place.blk * OWN + c
        here = jnp.sum(jnp.where(ids == own, named, 0.0), keepdims=True)
        rank = jnp.sum(jnp.where(ids < own, named, 0.0), keepdims=True)
        weights.append([here * jnp.where(jnp.abs(rank - s) < 0.5, 1.0, 0.0) for s in range(HOT)])
    return weights


def start_stage(src, got, sems, where, count):
    return [send(src, got.at[o - 1], sems, o - 1, where(o)) for o in range(1, count)]


def end_stage(copies, mine, got):
    for copy in copies:
        copy.wait()
    return add_up([mine.astype(jnp.float32)] + [got[o].astype(jnp.float32) for o in range(len(copies))])


def start_scatter(place, slots, got, sems):
    return [
        send(slots.at[(place.z + o) % NZ], got.at[o - 1], sems, o - 1, place.along_z(o)) for o in range(1, NZ)
    ]


def start_gather(place, mine, result, sems):
    copies = [send(mine, result.at[place.z], sems, o - 1, place.along_z(o)) for o in range(1, NZ)]
    result[place.z] = mine[...]
    return copies


def weighted(weights, values):
    return add_up([w * v.astype(jnp.float32) for w, v in zip(weights, values)])


class Terms:
    def __init__(self, x, kern, work, piv, inverse, right, ext, squares):
        self.x, self.kern, self.work, self.piv, self.inverse = x, kern, work, piv, inverse
        self.right, self.ext, self.squares = right, ext, squares
        self.joint, self.width = x.shape
        self.lead = self.joint - T

    def place_rows(self, k, mine, other):
        rs = slice(k * T, (k + 1) * T)
        self.x[rs, :T] = mine[:T].astype(jnp.bfloat16)
        self.x[rs, T:] = other[:T].astype(jnp.bfloat16)
        obs = jnp.broadcast_to(mine[T : T + 1], (T, T))
        self.work[rs, self.joint :] = jnp.transpose(obs)
        wide = self.x[rs, :].astype(jnp.float32)
        self.squares[rs, :] = jnp.broadcast_to(jnp.sum(wide * wide, axis=1, keepdims=True), (T, T))

    def covariance(self, rows, cols):
        start, stop = cols
        for k in rows:
            rs = slice(k * T, (k + 1) * T)
            gram = lax.dot_general(
                self.x[rs, :],
                self.x[start * T : stop * T, :],
                (((1,), (1,)), ((), ())),
                preferred_element_type=jnp.float32,
            )
            for m in range(start, stop):
                across = jnp.transpose(self.squares[m * T : (m + 1) * T, :])
                dist = self.squares[rs, :] + across - 2.0 * gram[:, (m - start) * T : (m - start + 1) * T]
                kern = jnp.exp(-dist * (0.5 / self.width))
                if m == k:
                    kern = jnp.where(diagonal(), 1.1, kern)
                self.kern[rs, m * T : (m + 1) * T] = kern
                self.work[rs, m * T : (m + 1) * T] = kern

    def near_first(self):
        for rows, cols in (((0, 1, 4), (0, 2)), ((0, 1, 4), (4, 5))):
            self.covariance(rows, cols)
        self.piv[...] = self.work[:T, :T]

    def near_pivot(self, k):
        w = self.work
        a, b = k * T, (k + 1) * T
        negative_inverse(self.piv)
        minv = -self.piv[...]
        self.inverse[k] = minv
        groups = [(self.lead, self.joint + T)]
        if k == 0:
            groups.append((T, 2 * T))
        for lo, hi in groups:
            t = dot32(minv, w[a:b, lo:hi])
            w[a:b, lo:hi] = t
            for r in range(k + 1, 2):
                w[r * T : (r + 1) * T, lo:hi] = w[r * T : (r + 1) * T, lo:hi] - dot32(w[r * T : (r + 1) * T, a:b], t)
            w[self.lead :, lo:hi] = w[self.lead :, lo:hi] - dot32(w[self.lead :, a:b], t)
        if k == 0:
            self.piv[...] = w[T : 2 * T, T : 2 * T]

    def finish(self):
        w, joint, lead = self.work, self.joint, self.lead
        self.covariance((2, 3), (0, 5))
        self.covariance((0, 1, 4), (2, 4))
        hot = slice(2 * T, lead)
        first = dot32(self.inverse[0], w[:T, hot])
        w[:T, hot] = first
        w[T:, hot] = w[T:, hot] - dot32(w[T:, :T], first)
        w[hot, T : 2 * T] = w[hot, T : 2 * T] - dot32(w[hot, :T], w[:T, T : 2 * T])
        w[hot, lead:] = w[hot, lead:] - dot32(w[hot, :T], w[:T, lead:])
        second = dot32(self.inverse[1], w[T : 2 * T, hot])
        w[T : 2 * T, hot] = second
        w[2 * T :, hot] = w[2 * T :, hot] - dot32(w[2 * T :, T : 2 * T], second)
        w[hot, lead:] = w[hot, lead:] - dot32(w[hot, T : 2 * T], w[T : 2 * T, lead:])
        for k in (2, 3):
            a, b = k * T, (k + 1) * T
            self.piv[...] = w[a:b, a:b]
            negative_inverse(self.piv)
            t = -dot32(self.piv[...], w[a:b, b:])
            w[b:, b:] = w[b:, b:] - dot32(w[b:, a:b], t)
            w[a:b, b:] = t
        right = self.right
        right[lead - T :, :] = w[lead - T : lead, lead:]
        for k in (2, 1, 0):
            a, b = k * T, (k + 1) * T
            right[a:b, :] = w[a:b, lead:] - dot32(w[a:b, b:lead], right[b:, :])
        self.piv[...] = w[lead:, lead:joint]
        res = w[lead:, joint:]
        logs = negative_inverse(self.piv)
        sinv = -self.piv[...]
        u = dot32(sinv, res)
        quad = jnp.sum(res * u, axis=0, keepdims=True)
        inner = sinv - u * jnp.transpose(u)
        lane = lax.broadcasted_iota(jnp.int32, (T, T), 1)
        for k in range(5):
            rs = slice(k * T, (k + 1) * T)
            e = -right[rs, :T] if k < 4 else jnp.where(diagonal(), 1.0, 0.0)
            alpha = right[rs, T:] if k < 4 else jnp.zeros((T, T), jnp.float32)
            v = dot32(e, u)
            self.ext[rs, :T] = e
            self.ext[rs, T:] = jnp.where(lane == 0, v, jnp.where(lane == 1, alpha, 0.0))
            w[rs, :T] = -dot32(e, inner)
            w[rs, T : 2 * T] = jnp.where(lane == 0, alpha, jnp.where(lane == 1, v, 0.0))
        return -0.5 * (quad + logs) - 0.5 * T * math.log(2.0 * math.pi)

    def grad_rows(self, k):
        rs = slice(k * T, (k + 1) * T)
        col = lax.broadcasted_iota(jnp.int32, (T, self.joint), 1)
        row = lax.broadcasted_iota(jnp.int32, (T, self.joint), 0)
        m = dot32(self.work[rs, : 2 * T], self.ext[...], ((1,), (1,)))
        sym = jnp.where(col == row + k * T, 0.0, m * self.kern[rs, :] * (-0.5 / self.width)).astype(jnp.bfloat16)
        rowsum = jnp.sum(sym.astype(jnp.float32), axis=1, keepdims=True)
        part = jnp.dot(sym, self.x[...], preferred_element_type=jnp.float32)
        return 2.0 * (rowsum * self.x[rs, :].astype(jnp.float32) - part)


def diagonal():
    return lax.broadcasted_iota(jnp.int32, (T, T), 0) == lax.broadcasted_iota(jnp.int32, (T, T), 1)


def whole_kernel(cond_ref, own_ref, value_ref, out_ref,
                 m0, m1, m2, mz, mx, my,
                 near_mine, near_other, hot_mine, hot_other, slots, zgot, xgot, ygot, held,
                 x, kern, work, piv, inverse, right, ext, squares,
                 back_mine, back_other, back_got, side_mine, side_other, side_got, near_out, near_got,
                 slots2, hot2, zgot2, xgot2, ygot2, held2,
                 msem, nsem, psem, zsem, xsem, ysem, gsem, fsem,
                 nsem2, psem2, zsem2, xsem2, ysem2, gsem2):
    place = Place()
    terms = Terms(x, kern, work, piv, inverse, right, ext, squares)
    place.greet()
    ids = lax.broadcasted_iota(jnp.int32, (G, T), 0) * T + lax.broadcasted_iota(jnp.int32, (G, T), 1)
    marks = jnp.zeros((G, T), jnp.float32)
    for c in range(OWN):
        for k in (2, 3):
            marks = jnp.where(ids == cond_ref[c, k], 1.0, marks)
    m0[...] = marks
    stage = start_stage(m0, mz, msem.at[:, pl.ds(0, NZ - 1)], place.along_z, NZ)
    near = []
    for by in (1, 2):
        near.append(send(own_ref, near_mine.at[pl.ds(by * OWN, OWN)], nsem, by - 1, place.along_blk(by)))
    early = [send(own_ref, near_other.at[pl.ds(0, OWN)], psem, 0, place.partner())]
    near_mine[:OWN] = own_ref[...]
    m1[...] = end_stage(stage, m0[...], mz)
    stage = start_stage(m1, mx, msem.at[:, pl.ds(NZ - 1, NX - 1)], place.along_x, NX)
    for by in (1, 2):
        near[by - 1].wait()
        part = pl.ds(by * OWN, OWN)
        early.append(send(near_mine.at[part], near_other.at[part], psem, by, place.partner()))
    m2[...] = end_stage(stage, m1[...], mx)
    stage = start_stage(m2, my, msem.at[:, pl.ds(NZ + NX - 2, NY - 1)], place.along_y, NY)
    marks = end_stage(stage, m2[...], my)
    picks = pick_weights(place, marks)
    for s in range(HOT):
        slots[s] = weighted([p[s] for p in picks], [own_ref[c] for c in range(OWN)]).astype(jnp.bfloat16)
    stage = start_scatter(place, slots, zgot, zsem)
    for copy in early:
        copy.wait()
    near_ids = []
    for s in range(OWN * (NEAR + 1)):
        near_ids.append((place.blk + NX * NZ * NY - s // OWN) % (NX * NZ * NY) * OWN + s % OWN)
    near_w = [[jnp.where(cond_ref[place.rep, k] == i, 1.0, 0.0) for i in near_ids] for k in range(2)]
    own_w = [jnp.where(place.rep == c, 1.0, 0.0) for c in range(OWN)]
    count = len(near_ids)
    for k in range(2):
        terms.place_rows(
            k,
            weighted(near_w[k], [near_mine[s] for s in range(count)]),
            weighted(near_w[k], [near_other[s] for s in range(count)]),
        )
    terms.place_rows(
        4,
        weighted(own_w, [near_mine[c] for c in range(OWN)]),
        weighted(own_w, [near_other[c] for c in range(OWN)]),
    )
    terms.near_first()
    terms.near_pivot(0)
    held[0] = end_stage(stage, slots[place.z], zgot).astype(held.dtype)
    stage = start_stage(held.at[0], xgot, xsem, place.along_x, NX)
    held[1] = end_stage(stage, held[0], xgot).astype(held.dtype)
    stage = start_stage(held.at[1], ygot, ysem, place.along_y, NY)
    held[2] = end_stage(stage, held[1], ygot).astype(held.dtype)
    stage = start_gather(place, held.at[2], hot_mine, gsem)
    passed = [send(held.at[2], hot_other.at[place.z], fsem, 0, place.partner())]
    terms.near_pivot(1)
    for o in range(1, NZ):
        stage[o - 1].wait()
        slot = (place.z + NZ - o) % NZ
        passed.append(send(hot_mine.at[slot], hot_other.at[slot], fsem, o, place.partner()))
    named = jnp.where(marks > 0.5, 1.0, 0.0)
    hot_w = []
    for k in (2, 3):
        rank = jnp.sum(jnp.where(ids < cond_ref[place.rep, k], named, 0.0), keepdims=True)
        hot_w.append([jnp.where(jnp.abs(rank - s) < 0.5, 1.0, 0.0) for s in range(HOT)])
    mine = [weighted(w, [hot_mine[s] for s in range(HOT)]) for w in hot_w]
    for copy in passed:
        copy.wait()
    for k in (0, 1):
        terms.place_rows(2 + k, mine[k], weighted(hot_w[k], [hot_other[s] for s in range(HOT)]))
    value_ref[...] = terms.finish()
    grads = [terms.grad_rows(k) for k in (2, 3)]
    for s in range(HOT):
        total = weighted([w[s] for w in hot_w], grads).astype(jnp.bfloat16)
        back_mine[s] = total[:, :T]
        back_other[s] = total[:, T:]
    hot_copy = send(back_other, back_got, psem2, 0, place.partner())
    grads = [terms.grad_rows(k) for k in (0, 1, 4)]
    for s in range(count):
        weights = [near_w[0][s], near_w[1][s]] + ([own_w[s]] if s < OWN else [])
        total = weighted(weights, grads).astype(jnp.bfloat16)
        side_mine[s] = total[:, :T]
        side_other[s] = total[:, T:]
    side_copy = send(side_other, side_got, psem2, 1, place.partner())
    hot_copy.wait()
    slots2[...] = (back_mine[...].astype(jnp.float32) + back_got[...].astype(jnp.float32)).astype(jnp.bfloat16)
    stage = start_scatter(place, slots2, zgot2, zsem2)
    side_copy.wait()
    part = pl.ds(OWN, OWN * NEAR)
    near_out[...] = (side_mine[part].astype(jnp.float32) + side_got[part].astype(jnp.float32)).astype(jnp.bfloat16)
    near = []
    for by in (1, 2):
        part = pl.ds((by - 1) * OWN, OWN)
        near.append(send(near_out.at[part], near_got.at[part], nsem2, by - 1, place.along_blk(-by)))
    held2[0] = end_stage(stage, slots2[place.z], zgot2).astype(held2.dtype)
    stage = start_stage(held2.at[0], xgot2, xsem2, place.along_x, NX)
    held2[1] = end_stage(stage, held2[0], xgot2).astype(held2.dtype)
    stage = start_stage(held2.at[1], ygot2, ysem2, place.along_y, NY)
    held2[2] = end_stage(stage, held2[1], ygot2).astype(held2.dtype)
    stage = start_gather(place, held2.at[2], hot2, gsem2)
    for copy in near:
        copy.wait()
    for c in range(OWN):
        total = side_mine[c].astype(jnp.float32) + side_got[c].astype(jnp.float32)
        for by in range(NEAR):
            total = total + near_got[by * OWN + c].astype(jnp.float32)
        out_ref[c * T : (c + 1) * T, :] = total
    for copy in stage:
        copy.wait()
    for c in range(OWN):
        rs = slice(c * T, (c + 1) * T)
        out_ref[rs, :] = out_ref[rs, :] + weighted(picks[c], [hot2[s] for s in range(HOT)])


def half(*shape):
    return pltpu.VMEM(shape, jnp.bfloat16)


def full(*shape):
    return pltpu.VMEM(shape, jnp.float32)


def dma(count):
    return pltpu.SemaphoreType.DMA((2, count))


def body(features, observations, cond_ids):
    per_dev = cond_ids.shape[0]
    width = features.shape[1]
    joint = (cond_ids.shape[1] + 1) * T
    count = OWN * (NEAR + 1)
    obs = jnp.broadcast_to(observations[:, None, :], (per_dev, PACK - T, T))
    own = jnp.concatenate([features.reshape(per_dev, T, width), obs], axis=1)
    ring = [NZ - 1, NX - 1, NY - 1]
    value, grad = pl.pallas_call(
        whole_kernel,
        out_shape=(
            jax.ShapeDtypeStruct((G, T), jnp.float32),
            jax.ShapeDtypeStruct((per_dev * T, width), jnp.float32),
        ),
        in_specs=[pl.BlockSpec(memory_space=pltpu.SMEM), VMEM],
        out_specs=(VMEM, VMEM),
        scratch_shapes=[full(G, T)] * 3
        + [full(n, G, T) for n in ring]
        + [half(count, PACK, T)] * 2
        + [half(HOT, PACK, T)] * 3
        + [half(n, PACK, T) for n in ring + [3]]
        + [
            half(joint, 2 * T),
            full(joint, joint),
            full(joint, joint + T),
            full(T, T),
            full(2, T, T),
            full(joint - T, 2 * T),
            full(joint, 2 * T),
            full(joint, T),
        ]
        + [half(HOT, T, T)] * 3
        + [half(count, T, T)] * 3
        + [half(OWN * NEAR, T, T)] * 2
        + [half(HOT, T, T)] * 2
        + [half(n, T, T) for n in ring + [3]]
        + [dma(n) for n in (sum(ring), NEAR, NEAR + 1, *ring, NZ - 1, NZ)]
        + [dma(n) for n in (NEAR, 2, *ring, NZ - 1)],
        compiler_params=pltpu.CompilerParams(
            collective_id=0, has_side_effects=True, vmem_limit_bytes=50 << 20
        ),
        name="block_vecchia",
    )(cond_ids, own)
    return (value[0, :1], grad)


def solution(mesh):
    placed = (P("blk", "rep"), P("blk", None), P("blk", None))
    return jax.shard_map(
        body,
        mesh=mesh,
        in_specs=placed,
        out_specs=(P(("blk", "rep")), P("blk", "rep")),
        check_vma=False,
    )
```

```python
import math

import jax
import jax.numpy as jnp
from jax import lax
from jax.experimental import pallas as pl
from jax.experimental.pallas import tpu as pltpu
from jax.sharding import PartitionSpec as P

HOT = 8
T = 128
G = 8
VMEM = pl.BlockSpec(memory_space=pltpu.VMEM)
HI = lax.Precision.HIGHEST


def dot32(a, b, dims=((1,), (0,))):
    return lax.dot_general(a, b, (dims, ((), ())), precision=HI, preferred_element_type=jnp.float32)


UNROLL = 8


def split(value):
    high = value.astype(jnp.bfloat16)
    return high, (value - high.astype(jnp.float32)).astype(jnp.bfloat16)


def add_up(terms):
    while len(terms) > 1:
        odd = terms[-1:] if len(terms) % 2 else []
        terms = [a + b for a, b in zip(terms[::2], terms[1::2])] + odd
    return terms[0]


def invert_rows(rows, s):
    prod = None
    inv = {}
    for k in range(0, G, 2):
        j = k + 1
        a, b, c = s[k, k], s[j, k], s[j, j]
        det = a * c - b * b
        prod = det if prod is None else prod * det
        r = 1.0 / det
        ra, rb, rc = a * r, b * r, c * r
        inv[k] = (ra, rb, rc)
        rest = [i for i in range(G) if i not in (k, j)]
        low = {}
        for m in range(j + 1, G):
            s[k, m], s[j, m] = s[m, k], s[m, j]
        for i in rest:
            p, q = s[i, k], s[i, j]
            low[i] = (p * rc - q * rb, q * ra - p * rb)
        for i in rest:
            for m in range(j + 1, G):
                if i < k or i >= m:
                    sk, sj = s[m, k], s[m, j]
                    s[i, m] = s[i, m] - (low[i][0] * sk + low[i][1] * sj)
        for i in rest:
            rows[i] = rows[i] - (low[i][0] * rows[k] + low[i][1] * rows[j])
    for k in range(0, G, 2):
        ra, rb, rc = inv[k]
        x, y = rows[k], rows[k + 1]
        rows[k], rows[k + 1] = rc * x - rb * y, ra * y - rb * x
    return prod


def negative_inverse(ref, half=False):
    lane = lax.broadcasted_iota(jnp.int32, (G, T), 1)
    sub = lax.broadcasted_iota(jnp.int32, (G, T), 0)
    count = T // G

    def groups(step, logs):
        blks = [ref[t * G : (t + 1) * G, :] for t in range(count)]
        for u in range(UNROLL):
            first = u * G
            inside = (lane >= first) & (lane < first + G)
            panel = blks[u]
            rows = []
            for k in range(G):
                row = jnp.broadcast_to(panel[k : k + 1, :], (G, T))
                rows.append(jnp.where(inside, jnp.where(lane == first + k, -1.0, 0.0), row))
            s = {}
            for k in range(G):
                col = jnp.broadcast_to(panel[:, first + k : first + k + 1], (G, T))
                for i in range(k, G):
                    s[i, k] = jnp.broadcast_to(col[i : i + 1, :], (G, T))
                    s[k, i] = s[i, k]
            prod = invert_rows(rows, s)
            logs = logs + jnp.log(prod)
            order = [(u + d) % count for d in range(1, count)]
            for t in order:
                old = blks[t]
                terms = [
                    jnp.broadcast_to(old[:, first + k : first + k + 1], (G, T)) * rows[k] for k in range(G)
                ]
                blks[t] = jnp.where(inside, 0.0, old) - add_up(terms)
            top = rows[0]
            for k in range(1, G):
                top = jnp.where(sub == k, rows[k], top)
            blks[u] = top
        shift = UNROLL * G
        for t in range(count):
            at = (t - UNROLL) % count
            ref[at * G : (at + 1) * G, :] = blks[t] if shift == T else pltpu.roll(blks[t], T - shift, 1)
        return logs

    steps = count // UNROLL
    return lax.fori_loop(0, steps // 2 if half else steps, groups, jnp.zeros((G, T), jnp.float32))


NX, NZ, NY = 4, 8, 4
NEAR = 2
OWN = 2
PACK = T + 16
MESH = pl.DeviceIdType.MESH


class Place:
    def __init__(self):
        self.blk = lax.axis_index("blk")
        self.rep = lax.axis_index("rep")
        self.x = self.blk % NX
        self.z = self.blk // NX % NZ
        self.y = self.blk // (NX * NZ)

    def along_x(self, by):
        return self.blk - self.x + (self.x + by) % NX, self.rep

    def along_z(self, by):
        return self.blk + ((self.z + by) % NZ - self.z) * NX, self.rep

    def along_xy(self, by):
        x, y = by % NX, by // NX
        return ((self.y + y) % NY * NZ + self.z) * NX + (self.x + x) % NX, self.rep

    def along_y(self, by):
        return (self.blk + by * NX * NZ) % (NX * NZ * NY), self.rep

    def along_blk(self, by):
        return (self.blk + by) % (NX * NZ * NY), self.rep

    def partner(self):
        return self.blk, 1 - self.rep

    def greet(self):
        there = [self.along_z(o) for o in range(1, NZ)]
        there += [self.along_xy(o) for o in range(1, NX * NY)]
        there += [self.along_blk(o) for o in (1, 2, -1, -2)]
        there += [self.partner()]
        barrier = pltpu.get_barrier_semaphore()
        for device in there:
            pl.semaphore_signal(barrier, inc=1, device_id=device, device_id_type=MESH)
        return len(there)

    def meet(self, count):
        pl.semaphore_wait(pltpu.get_barrier_semaphore(), count)


def send(src, dst, sems, index, device):
    copy = pltpu.make_async_remote_copy(
        src_ref=src,
        dst_ref=dst,
        send_sem=sems.at[0, index],
        recv_sem=sems.at[1, index],
        device_id=device,
        device_id_type=MESH,
    )
    copy.start()
    return copy


def pick_weights(first, marks):
    ids = lax.broadcasted_iota(jnp.int32, (G, T), 0) * T + lax.broadcasted_iota(jnp.int32, (G, T), 1)
    named = jnp.where(marks > 0.5, 1.0, 0.0)
    weights = []
    for c in range(OWN):
        own = first + c
        here = jnp.sum(jnp.where(ids == own, named, 0.0), keepdims=True)
        rank = jnp.sum(jnp.where(ids < own, named, 0.0), keepdims=True)
        weights.append([here * jnp.where(jnp.abs(rank - s) < 0.5, 1.0, 0.0) for s in range(HOT)])
    return weights


def start_stage(src, got, sems, where, count):
    return [send(src, got.at[o - 1], sems, o - 1, where(o)) for o in range(1, count)]


def end_stage(copies, mine, got):
    for copy in copies:
        copy.wait()
    return add_up([mine.astype(jnp.float32)] + [got[o].astype(jnp.float32) for o in range(len(copies))])


def start_scatter(place, slots, got, sems):
    return [
        send(slots.at[(place.z + o) % NZ], got.at[o - 1], sems, o - 1, place.along_z(o)) for o in range(1, NZ)
    ]


def start_gather(place, mine, result, sems):
    copies = [send(mine, result.at[place.z], sems, o - 1, place.along_z(o)) for o in range(1, NZ)]
    result[place.z] = mine[...]
    return copies


def weighted(weights, values):
    return add_up([w * v.astype(jnp.float32) for w, v in zip(weights, values)])


class Terms:
    def __init__(self, x, kern, work, piv, inverse, right, ext, squares):
        self.x, self.kern, self.work, self.piv, self.inverse = x, kern, work, piv, inverse
        self.right, self.ext, self.squares = right, ext, squares
        self.joint, self.width = x.shape
        self.lead = self.joint - T

    def place_rows(self, k, mine, other, line=None):
        rs = slice(k * T, (k + 1) * T)
        self.x[rs, :T] = mine[:T].astype(jnp.bfloat16)
        self.x[rs, T:] = other[:T].astype(jnp.bfloat16)
        obs = jnp.broadcast_to(mine[T : T + 1] if line is None else line, (T, T))
        self.work[rs, self.joint :] = jnp.transpose(obs)
        wide = self.x[rs, :].astype(jnp.float32)
        self.squares[rs, :] = jnp.broadcast_to(jnp.sum(wide * wide, axis=1, keepdims=True), (T, T))

    def covariance(self, rows, cols):
        start, stop = cols
        for k in rows:
            rs = slice(k * T, (k + 1) * T)
            gram = lax.dot_general(
                self.x[rs, :],
                self.x[start * T : stop * T, :],
                (((1,), (1,)), ((), ())),
                preferred_element_type=jnp.float32,
            )
            for m in range(start, stop):
                across = jnp.transpose(self.squares[m * T : (m + 1) * T, :])
                dist = self.squares[rs, :] + across - 2.0 * gram[:, (m - start) * T : (m - start + 1) * T]
                kern = jnp.exp(-dist * (0.5 / self.width))
                if m == k:
                    kern = jnp.where(diagonal(), 1.1, kern)
                self.kern[rs, m * T : (m + 1) * T] = kern
                self.work[rs, m * T : (m + 1) * T] = kern

    def near_first(self):
        for rows, cols in (((0, 1, 4), (0, 2)), ((0, 1, 4), (4, 5))):
            self.covariance(rows, cols)
        self.piv[...] = self.work[:T, :T]

    def near_pivot(self, k, half=False):
        w = self.work
        a, b = k * T, (k + 1) * T
        negative_inverse(self.piv, half)
        minv = -self.piv[...]
        self.inverse[k] = minv
        groups = [(self.lead, self.joint + T)]
        if k == 0:
            groups.append((T, 2 * T))
        for lo, hi in groups:
            t = dot32(minv, w[a:b, lo:hi])
            w[a:b, lo:hi] = t
            for r in range(k + 1, 2):
                w[r * T : (r + 1) * T, lo:hi] = w[r * T : (r + 1) * T, lo:hi] - dot32(w[r * T : (r + 1) * T, a:b], t)
            w[self.lead :, lo:hi] = w[self.lead :, lo:hi] - dot32(w[self.lead :, a:b], t)
        if k == 0:
            self.piv[...] = w[T : 2 * T, T : 2 * T]

    def finish(self):
        w, joint, lead = self.work, self.joint, self.lead
        self.covariance((2, 3), (0, 5))
        self.covariance((0, 1, 4), (2, 4))
        hot = slice(2 * T, lead)
        first = dot32(self.inverse[0], w[:T, hot])
        w[:T, hot] = first
        w[T:, hot] = w[T:, hot] - dot32(w[T:, :T], first)
        w[hot, T : 2 * T] = w[hot, T : 2 * T] - dot32(w[hot, :T], w[:T, T : 2 * T])
        w[hot, lead:] = w[hot, lead:] - dot32(w[hot, :T], w[:T, lead:])
        second = dot32(self.inverse[1], w[T : 2 * T, hot])
        w[T : 2 * T, hot] = second
        w[2 * T :, hot] = w[2 * T :, hot] - dot32(w[2 * T :, T : 2 * T], second)
        w[hot, lead:] = w[hot, lead:] - dot32(w[hot, T : 2 * T], w[T : 2 * T, lead:])
        for k in (2, 3):
            a, b = k * T, (k + 1) * T
            self.piv[...] = w[a:b, a:b]
            negative_inverse(self.piv)
            t = -dot32(self.piv[...], w[a:b, b:])
            w[b:, b:] = w[b:, b:] - dot32(w[b:, a:b], t)
            w[a:b, b:] = t
        right = self.right
        right[lead - T :, :] = w[lead - T : lead, lead:]
        for k in (2, 1, 0):
            a, b = k * T, (k + 1) * T
            right[a:b, :] = w[a:b, lead:] - dot32(w[a:b, b:lead], right[b:, :])
        self.piv[...] = w[lead:, lead:joint]
        res = w[lead:, joint:]
        logs = negative_inverse(self.piv)
        sinv = -self.piv[...]
        u = dot32(sinv, res)
        quad = jnp.sum(res * u, axis=0, keepdims=True)
        inner = sinv - u * jnp.transpose(u)
        lane = lax.broadcasted_iota(jnp.int32, (T, T), 1)
        for k in range(5):
            rs = slice(k * T, (k + 1) * T)
            e = -right[rs, :T] if k < 4 else jnp.where(diagonal(), 1.0, 0.0)
            alpha = right[rs, T:] if k < 4 else jnp.zeros((T, T), jnp.float32)
            v = dot32(e, u)
            left = (-dot32(e, inner), jnp.where(lane == 0, alpha, jnp.where(lane == 1, v, 0.0)))
            for i, term in enumerate(left + (e, jnp.where(lane == 0, v, jnp.where(lane == 1, alpha, 0.0)))):
                cols = slice(i % 2 * T, (i % 2 + 1) * T)
                self.ext[i // 2 * 2, rs, cols], self.ext[i // 2 * 2 + 1, rs, cols] = split(term)
        return -0.5 * (quad + logs) - 0.5 * T * math.log(2.0 * math.pi)

    def grad_rows(self, k):
        rs = slice(k * T, (k + 1) * T)
        col = lax.broadcasted_iota(jnp.int32, (T, self.joint), 1)
        row = lax.broadcasted_iota(jnp.int32, (T, self.joint), 0)
        across = (((1,), (1,)), ((), ()))
        m = add_up(
            [
                lax.dot_general(self.ext[i, rs, :], self.ext[j], across, preferred_element_type=jnp.float32)
                for i, j in ((0, 3), (1, 2), (0, 2))
            ]
        )
        sym = jnp.where(col == row + k * T, 0.0, m * self.kern[rs, :] * (-0.5 / self.width)).astype(jnp.bfloat16)
        rowsum = jnp.sum(sym.astype(jnp.float32), axis=1, keepdims=True)
        part = jnp.dot(sym, self.x[...], preferred_element_type=jnp.float32)
        return 2.0 * (rowsum * self.x[rs, :].astype(jnp.float32) - part)


def diagonal():
    return lax.broadcasted_iota(jnp.int32, (T, T), 0) == lax.broadcasted_iota(jnp.int32, (T, T), 1)


def whole_kernel(cond_ref, feat_ref, obs_ref, value_ref, out_ref,
                 m0, m1, mz, mxy, own, row, obs0, obs1, obs2, oz, oy, ox,
                 near_mine, near_other, hot_mine, hot_other, slots, zgot, ygot, held, whole,
                 x, kern, work, piv, inverse, right, ext, squares,
                 back_mine, back_other, back_got, side_mine, side_other, side_got, near_out, near_got,
                 slots2, hot2, zgot2, xgot2, ygot2, held2,
                 msem, rsem, osem, nsem, psem, zsem, ysem, xsem, gsem, fsem,
                 nsem2, psem2, zsem2, xsem2, ysem2, gsem2):
    place = Place()
    terms = Terms(x, kern, work, piv, inverse, right, ext, squares)
    greeted = place.greet()
    ids = lax.broadcasted_iota(jnp.int32, (G, T), 0) * T + lax.broadcasted_iota(jnp.int32, (G, T), 1)
    marks = jnp.zeros((G, T), jnp.float32)
    for c in range(OWN):
        for k in (2, 3):
            marks = jnp.where(ids == cond_ref[c, k], 1.0, marks)
    m0[...] = marks
    obs_rows = obs_ref[...].astype(jnp.float32)
    for c in range(OWN):
        own[c, :T, :] = feat_ref[c * T : (c + 1) * T, :]
        own[c, T:, :] = jnp.broadcast_to(obs_rows[c : c + 1, :], (PACK - T, T)).astype(jnp.bfloat16)
    near_mine[:OWN] = own[...]
    for c in range(OWN):
        row[NX - 1, c * T : (c + 1) * T, :] = feat_ref[c * T : (c + 1) * T, :]
    place.meet(greeted)
    stage = start_stage(m0, mz, msem.at[:, pl.ds(0, NZ - 1)], place.along_z, NZ)
    rows = start_stage(feat_ref, row, rsem, place.along_x, NX)
    near = []
    for by in (1, 2):
        near.append(send(own, near_mine.at[pl.ds(by * OWN, OWN)], nsem, by - 1, place.along_blk(by)))
    early = [send(own, near_other.at[pl.ds(0, OWN)], psem, 0, place.partner())]
    m1[...] = end_stage(stage, m0[...], mz)
    stage = start_stage(m1, mxy, msem.at[:, pl.ds(NZ - 1, NX * NY - 1)], place.along_xy, NX * NY)
    for by in (1, 2):
        near[by - 1].wait()
        part = pl.ds(by * OWN, OWN)
        early.append(send(near_mine.at[part], near_other.at[part], psem, by, place.partner()))
    near_ids = []
    for s in range(OWN * (NEAR + 1)):
        near_ids.append((place.blk + NX * NZ * NY - s // OWN) % (NX * NZ * NY) * OWN + s % OWN)
    near_w = [[jnp.where(cond_ref[place.rep, k] == i, 1.0, 0.0) for i in near_ids] for k in range(2)]
    own_w = [jnp.where(place.rep == c, 1.0, 0.0) for c in range(OWN)]
    count = len(near_ids)
    early[0].wait()
    terms.place_rows(
        4,
        weighted(own_w, [near_mine[c] for c in range(OWN)]),
        weighted(own_w, [near_other[c] for c in range(OWN)]),
    )
    for copy in early[1:]:
        copy.wait()
    for k in range(2):
        terms.place_rows(
            k,
            weighted(near_w[k], [near_mine[s] for s in range(count)]),
            weighted(near_w[k], [near_other[s] for s in range(count)]),
        )
    terms.near_first()
    marks = end_stage(stage, m1[...], mxy)
    for copy in rows:
        copy.wait()
    quarter = pl.ds(place.x * (T // NX), T // NX)
    picks = pick_weights(place.blk * OWN, marks)
    row_picks = [picks]
    blocks = [row[NX - 1, pl.ds(c * T + place.x * (T // NX), T // NX), :] for c in range(OWN)]
    for o in range(1, NX):
        row_picks.append(pick_weights(place.along_x(NX - o)[0] * OWN, marks))
        blocks += [row[o - 1, pl.ds(c * T + place.x * (T // NX), T // NX), :] for c in range(OWN)]
    for s in range(HOT):
        slots[s] = weighted([p[s] for ps in row_picks for p in ps], blocks).astype(jnp.bfloat16)
    obs = jnp.zeros((HOT, T), jnp.float32)
    for s in range(HOT):
        line = weighted([p[s] for p in picks], [obs_rows[c : c + 1, :] for c in range(OWN)])
        obs = jnp.where(lax.broadcasted_iota(jnp.int32, (HOT, T), 0) == s, line, obs)
    obs0[...] = obs
    stage = start_scatter(place, slots, zgot, zsem)
    obs_stage = start_stage(obs0, oz, osem.at[:, pl.ds(0, NZ - 1)], place.along_z, NZ)
    named = jnp.where(marks > 0.5, 1.0, 0.0)
    hot_w = []
    for k in (2, 3):
        rank = jnp.sum(jnp.where(ids < cond_ref[place.rep, k], named, 0.0), keepdims=True)
        hot_w.append([jnp.where(jnp.abs(rank - s) < 0.5, 1.0, 0.0) for s in range(HOT)])
    negative_inverse(piv, half=True)
    held[0] = end_stage(stage, slots[place.z], zgot).astype(held.dtype)
    obs1[...] = end_stage(obs_stage, obs0[...], oz)
    stage = start_stage(held.at[0], ygot, ysem, place.along_y, NY)
    obs_stage = start_stage(obs1, oy, osem.at[:, pl.ds(NZ - 1, NY - 1)], place.along_y, NY)
    terms.near_pivot(0, half=True)
    held[1] = end_stage(stage, held[0], ygot).astype(held.dtype)
    obs2[...] = end_stage(obs_stage, obs1[...], oy)
    whole[quarter, :] = held[1]
    stage = [send(held.at[1], whole.at[quarter], xsem, o - 1, place.along_x(o)) for o in range(1, NX)]
    obs_stage = start_stage(obs2, ox, osem.at[:, pl.ds(NZ + NY - 2, NX - 1)], place.along_x, NX)
    negative_inverse(piv, half=True)
    for copy in stage:
        copy.wait()
    hot_obs = end_stage(obs_stage, obs2[...], ox)
    stage = start_gather(place, whole, hot_mine, gsem)
    passed = [send(whole, hot_other.at[place.z], fsem, 0, place.partner())]
    terms.near_pivot(1, half=True)
    for o in range(1, NZ):
        stage[o - 1].wait()
        slot = (place.z + NZ - o) % NZ
        passed.append(send(hot_mine.at[slot], hot_other.at[slot], fsem, o, place.partner()))
    mine = [weighted(w, [hot_mine[s] for s in range(HOT)]) for w in hot_w]
    lines = [weighted(w, [hot_obs[s : s + 1, :] for s in range(HOT)]) for w in hot_w]
    for copy in passed:
        copy.wait()
    for k in (0, 1):
        terms.place_rows(2 + k, mine[k], weighted(hot_w[k], [hot_other[s] for s in range(HOT)]), lines[k])
    value_ref[...] = terms.finish()
    grads = [terms.grad_rows(k) for k in (2, 3)]
    for s in range(HOT):
        total = weighted([w[s] for w in hot_w], grads).astype(jnp.bfloat16)
        back_mine[s] = total[:, :T]
        back_other[s] = total[:, T:]
    hot_copy = send(back_other, back_got, psem2, 0, place.partner())
    grads = [terms.grad_rows(0)]
    hot_copy.wait()
    slots2[...] = (back_mine[...].astype(jnp.float32) + back_got[...].astype(jnp.float32)).astype(jnp.bfloat16)
    stage = start_scatter(place, slots2, zgot2, zsem2)
    grads += [terms.grad_rows(k) for k in (1, 4)]
    for s in range(count):
        weights = [near_w[0][s], near_w[1][s]] + ([own_w[s]] if s < OWN else [])
        total = weighted(weights, grads).astype(jnp.bfloat16)
        side_mine[s] = total[:, :T]
        side_other[s] = total[:, T:]
    side_copy = send(side_other, side_got, psem2, 1, place.partner())
    side_copy.wait()
    part = pl.ds(OWN, OWN * NEAR)
    near_out[...] = (side_mine[part].astype(jnp.float32) + side_got[part].astype(jnp.float32)).astype(jnp.bfloat16)
    near = []
    for by in (1, 2):
        part = pl.ds((by - 1) * OWN, OWN)
        near.append(send(near_out.at[part], near_got.at[part], nsem2, by - 1, place.along_blk(-by)))
    held2[0] = end_stage(stage, slots2[place.z], zgot2).astype(held2.dtype)
    stage = start_stage(held2.at[0], xgot2, xsem2, place.along_x, NX)
    held2[1] = end_stage(stage, held2[0], xgot2).astype(held2.dtype)
    stage = start_stage(held2.at[1], ygot2, ysem2, place.along_y, NY)
    held2[2] = end_stage(stage, held2[1], ygot2).astype(held2.dtype)
    stage = start_gather(place, held2.at[2], hot2, gsem2)
    for copy in near:
        copy.wait()
    for c in range(OWN):
        total = side_mine[c].astype(jnp.float32) + side_got[c].astype(jnp.float32)
        for by in range(NEAR):
            total = total + near_got[by * OWN + c].astype(jnp.float32)
        out_ref[c * T : (c + 1) * T, :] = total
    for copy in stage:
        copy.wait()
    for c in range(OWN):
        rs = slice(c * T, (c + 1) * T)
        out_ref[rs, :] = out_ref[rs, :] + weighted(picks[c], [hot2[s] for s in range(HOT)])


def half(*shape):
    return pltpu.VMEM(shape, jnp.bfloat16)


def full(*shape):
    return pltpu.VMEM(shape, jnp.float32)


def dma(count):
    return pltpu.SemaphoreType.DMA((2, count))


def body(features, observations, cond_ids):
    per_dev = cond_ids.shape[0]
    width = features.shape[1]
    joint = (cond_ids.shape[1] + 1) * T
    count = OWN * (NEAR + 1)
    ring = [NZ - 1, NX - 1, NY - 1]
    value, grad = pl.pallas_call(
        whole_kernel,
        out_shape=(
            jax.ShapeDtypeStruct((G, T), jnp.float32),
            jax.ShapeDtypeStruct((per_dev * T, width), jnp.float32),
        ),
        in_specs=[pl.BlockSpec(memory_space=pltpu.SMEM), VMEM, VMEM],
        out_specs=(VMEM, VMEM),
        scratch_shapes=[full(G, T)] * 2
        + [full(n, G, T) for n in (NZ - 1, NX * NY - 1)]
        + [half(OWN, PACK, T), half(NX, OWN * T, T)]
        + [full(HOT, T)] * 3
        + [full(n - 1, HOT, T) for n in (NZ, NY, NX)]
        + [half(count, PACK, T)] * 2
        + [half(HOT, T, T)] * 2
        + [half(n, T // NX, T) for n in (HOT, NZ - 1, NY - 1, 2)]
        + [half(T, T)]
        + [
            half(joint, 2 * T),
            full(joint, joint),
            full(joint, joint + T),
            full(T, T),
            full(2, T, T),
            full(joint - T, 2 * T),
            half(4, joint, 2 * T),
            full(joint, T),
        ]
        + [half(HOT, T, T)] * 3
        + [half(count, T, T)] * 3
        + [half(OWN * NEAR, T, T)] * 2
        + [half(HOT, T, T)] * 2
        + [half(n, T, T) for n in ring + [3]]
        + [dma(n) for n in (NZ + NX * NY - 2, NX - 1, sum(ring), NEAR, NEAR + 1)]
        + [dma(n) for n in (NZ - 1, NY - 1, NX - 1, NZ - 1, NZ)]
        + [dma(n) for n in (NEAR, 2, *ring, NZ - 1)],
        compiler_params=pltpu.CompilerParams(
            collective_id=0, has_side_effects=True, vmem_limit_bytes=50 << 20
        ),
        name="block_vecchia",
    )(cond_ids, features, observations)
    return (value[0, :1], grad)


def solution(mesh):
    placed = (P("blk", "rep"), P("blk", None), P("blk", None))
    return jax.shard_map(
        body,
        mesh=mesh,
        in_specs=placed,
        out_specs=(P(("blk", "rep")), P("blk", "rep")),
        check_vma=False,
    )
```

```python
import math

import jax
import jax.numpy as jnp
from jax import lax
from jax.experimental import pallas as pl
from jax.experimental.pallas import tpu as pltpu
from jax.sharding import PartitionSpec as P

HOT = 8
T = 128
G = 8
VMEM = pl.BlockSpec(memory_space=pltpu.VMEM)
HI = lax.Precision.HIGHEST


def dot32(a, b, dims=((1,), (0,))):
    return lax.dot_general(a, b, (dims, ((), ())), precision=HI, preferred_element_type=jnp.float32)


UNROLL = 8


def split(value):
    high = value.astype(jnp.bfloat16)
    return high, (value - high.astype(jnp.float32)).astype(jnp.bfloat16)


def add_up(terms):
    while len(terms) > 1:
        odd = terms[-1:] if len(terms) % 2 else []
        terms = [a + b for a, b in zip(terms[::2], terms[1::2])] + odd
    return terms[0]


def invert_rows(rows, s):
    prod = None
    inv = {}
    for k in range(0, G, 2):
        j = k + 1
        a, b, c = s[k, k], s[j, k], s[j, j]
        det = a * c - b * b
        prod = det if prod is None else prod * det
        r = 1.0 / det
        ra, rb, rc = a * r, b * r, c * r
        inv[k] = (ra, rb, rc)
        rest = [i for i in range(G) if i not in (k, j)]
        low = {}
        for m in range(j + 1, G):
            s[k, m], s[j, m] = s[m, k], s[m, j]
        for i in rest:
            p, q = s[i, k], s[i, j]
            low[i] = (p * rc - q * rb, q * ra - p * rb)
        for i in rest:
            for m in range(j + 1, G):
                if i < k or i >= m:
                    sk, sj = s[m, k], s[m, j]
                    s[i, m] = s[i, m] - (low[i][0] * sk + low[i][1] * sj)
        for i in rest:
            rows[i] = rows[i] - (low[i][0] * rows[k] + low[i][1] * rows[j])
    for k in range(0, G, 2):
        ra, rb, rc = inv[k]
        x, y = rows[k], rows[k + 1]
        rows[k], rows[k + 1] = rc * x - rb * y, ra * y - rb * x
    return prod


def negative_inverse(ref, half=False):
    lane = lax.broadcasted_iota(jnp.int32, (G, T), 1)
    sub = lax.broadcasted_iota(jnp.int32, (G, T), 0)
    count = T // G

    def groups(step, logs):
        blks = [ref[t * G : (t + 1) * G, :] for t in range(count)]
        for u in range(UNROLL):
            first = u * G
            inside = (lane >= first) & (lane < first + G)
            panel = blks[u]
            rows = []
            for k in range(G):
                row = jnp.broadcast_to(panel[k : k + 1, :], (G, T))
                rows.append(jnp.where(inside, jnp.where(lane == first + k, -1.0, 0.0), row))
            s = {}
            for k in range(G):
                col = jnp.broadcast_to(panel[:, first + k : first + k + 1], (G, T))
                for i in range(k, G):
                    s[i, k] = jnp.broadcast_to(col[i : i + 1, :], (G, T))
                    s[k, i] = s[i, k]
            prod = invert_rows(rows, s)
            logs = logs + jnp.log(prod)
            order = [(u + d) % count for d in range(1, count)]
            for t in order:
                old = blks[t]
                terms = [
                    jnp.broadcast_to(old[:, first + k : first + k + 1], (G, T)) * rows[k] for k in range(G)
                ]
                blks[t] = jnp.where(inside, 0.0, old) - add_up(terms)
            top = rows[0]
            for k in range(1, G):
                top = jnp.where(sub == k, rows[k], top)
            blks[u] = top
        shift = UNROLL * G
        for t in range(count):
            at = (t - UNROLL) % count
            ref[at * G : (at + 1) * G, :] = blks[t] if shift == T else pltpu.roll(blks[t], T - shift, 1)
        return logs

    steps = count // UNROLL
    return lax.fori_loop(0, steps // 2 if half else steps, groups, jnp.zeros((G, T), jnp.float32))


NX, NZ, NY = 4, 8, 4
NEAR = 2
OWN = 2
PACK = T + 16
MESH = pl.DeviceIdType.MESH


class Place:
    def __init__(self):
        self.blk = lax.axis_index("blk")
        self.rep = lax.axis_index("rep")
        self.x = self.blk % NX
        self.z = self.blk // NX % NZ
        self.y = self.blk // (NX * NZ)

    def along_x(self, by):
        return self.blk - self.x + (self.x + by) % NX, self.rep

    def along_z(self, by):
        return self.blk + ((self.z + by) % NZ - self.z) * NX, self.rep

    def along_xy(self, by):
        x, y = by % NX, by // NX
        return ((self.y + y) % NY * NZ + self.z) * NX + (self.x + x) % NX, self.rep

    def along_y(self, by):
        return (self.blk + by * NX * NZ) % (NX * NZ * NY), self.rep

    def along_blk(self, by):
        return (self.blk + by) % (NX * NZ * NY), self.rep

    def partner(self):
        return self.blk, 1 - self.rep

    def greet(self):
        there = [self.along_z(o) for o in range(1, NZ)]
        there += [self.along_xy(o) for o in range(1, NX * NY)]
        there += [self.along_blk(o) for o in (1, 2, -1, -2)]
        there += [self.partner()]
        barrier = pltpu.get_barrier_semaphore()
        for device in there:
            pl.semaphore_signal(barrier, inc=1, device_id=device, device_id_type=MESH)
        return len(there)

    def meet(self, count):
        pl.semaphore_wait(pltpu.get_barrier_semaphore(), count)


def send(src, dst, sems, index, device):
    copy = pltpu.make_async_remote_copy(
        src_ref=src,
        dst_ref=dst,
        send_sem=sems.at[0, index],
        recv_sem=sems.at[1, index],
        device_id=device,
        device_id_type=MESH,
    )
    copy.start()
    return copy


def pick_weights(first, marks):
    ids = lax.broadcasted_iota(jnp.int32, (G, T), 0) * T + lax.broadcasted_iota(jnp.int32, (G, T), 1)
    named = jnp.where(marks > 0.5, 1.0, 0.0)
    weights = []
    for c in range(OWN):
        own = first + c
        here = jnp.sum(jnp.where(ids == own, named, 0.0), keepdims=True)
        rank = jnp.sum(jnp.where(ids < own, named, 0.0), keepdims=True)
        weights.append([here * jnp.where(jnp.abs(rank - s) < 0.5, 1.0, 0.0) for s in range(HOT)])
    return weights


def start_stage(src, got, sems, where, count):
    return [send(src, got.at[o - 1], sems, o - 1, where(o)) for o in range(1, count)]


def end_stage(copies, mine, got):
    for copy in copies:
        copy.wait()
    return add_up([mine.astype(jnp.float32)] + [got[o].astype(jnp.float32) for o in range(len(copies))])


def start_scatter(place, slots, got, sems):
    return [
        send(slots.at[(place.z + o) % NZ], got.at[o - 1], sems, o - 1, place.along_z(o)) for o in range(1, NZ)
    ]


def start_gather(place, mine, result, sems):
    copies = [send(mine, result.at[place.z], sems, o - 1, place.along_z(o)) for o in range(1, NZ)]
    result[place.z] = mine[...]
    return copies


def weighted(weights, values):
    return add_up([w * v.astype(jnp.float32) for w, v in zip(weights, values)])


class Terms:
    def __init__(self, x, kern, work, piv, inverse, right, ext, squares):
        self.x, self.kern, self.work, self.piv, self.inverse = x, kern, work, piv, inverse
        self.right, self.ext, self.squares = right, ext, squares
        self.joint, self.width = x.shape
        self.lead = self.joint - T

    def place_rows(self, k, mine, other, line=None):
        rs = slice(k * T, (k + 1) * T)
        self.x[rs, :T] = mine[:T].astype(jnp.bfloat16)
        self.x[rs, T:] = other[:T].astype(jnp.bfloat16)
        obs = jnp.broadcast_to(mine[T : T + 1] if line is None else line, (T, T))
        self.work[rs, self.joint :] = jnp.transpose(obs)
        wide = self.x[rs, :].astype(jnp.float32)
        self.squares[rs, :] = jnp.broadcast_to(jnp.sum(wide * wide, axis=1, keepdims=True), (T, T))

    def covariance(self, rows, cols):
        start, stop = cols
        for k in rows:
            rs = slice(k * T, (k + 1) * T)
            gram = lax.dot_general(
                self.x[rs, :],
                self.x[start * T : stop * T, :],
                (((1,), (1,)), ((), ())),
                preferred_element_type=jnp.float32,
            )
            for m in range(start, stop):
                across = jnp.transpose(self.squares[m * T : (m + 1) * T, :])
                dist = self.squares[rs, :] + across - 2.0 * gram[:, (m - start) * T : (m - start + 1) * T]
                kern = jnp.exp(-dist * (0.5 / self.width))
                if m == k:
                    kern = jnp.where(diagonal(), 1.1, kern)
                self.kern[rs, m * T : (m + 1) * T] = kern
                self.work[rs, m * T : (m + 1) * T] = kern

    def near_first(self):
        for rows, cols in (((0, 1, 4), (0, 2)), ((0, 1, 4), (4, 5))):
            self.covariance(rows, cols)
        self.piv[...] = self.work[:T, :T]

    def near_update(self, k):
        w = self.work
        a, b = k * T, (k + 1) * T
        minv = -self.piv[...]
        self.inverse[k] = minv
        groups = [(self.lead, self.joint + T)]
        if k == 0:
            groups.append((T, 2 * T))
        for lo, hi in groups:
            t = dot32(minv, w[a:b, lo:hi])
            w[a:b, lo:hi] = t
            for r in range(k + 1, 2):
                w[r * T : (r + 1) * T, lo:hi] = w[r * T : (r + 1) * T, lo:hi] - dot32(w[r * T : (r + 1) * T, a:b], t)
            w[self.lead :, lo:hi] = w[self.lead :, lo:hi] - dot32(w[self.lead :, a:b], t)
        if k == 0:
            self.piv[...] = w[T : 2 * T, T : 2 * T]

    def finish(self):
        w, joint, lead = self.work, self.joint, self.lead
        self.covariance((2, 3), (0, 5))
        self.covariance((0, 1, 4), (2, 4))
        hot = slice(2 * T, lead)
        first = dot32(self.inverse[0], w[:T, hot])
        w[:T, hot] = first
        w[T:, hot] = w[T:, hot] - dot32(w[T:, :T], first)
        w[hot, T : 2 * T] = w[hot, T : 2 * T] - dot32(w[hot, :T], w[:T, T : 2 * T])
        w[hot, lead:] = w[hot, lead:] - dot32(w[hot, :T], w[:T, lead:])
        second = dot32(self.inverse[1], w[T : 2 * T, hot])
        w[T : 2 * T, hot] = second
        w[2 * T :, hot] = w[2 * T :, hot] - dot32(w[2 * T :, T : 2 * T], second)
        w[hot, lead:] = w[hot, lead:] - dot32(w[hot, T : 2 * T], w[T : 2 * T, lead:])
        for k in (2, 3):
            a, b = k * T, (k + 1) * T
            self.piv[...] = w[a:b, a:b]
            negative_inverse(self.piv)
            t = -dot32(self.piv[...], w[a:b, b:])
            w[b:, b:] = w[b:, b:] - dot32(w[b:, a:b], t)
            w[a:b, b:] = t
        right = self.right
        right[lead - T :, :] = w[lead - T : lead, lead:]
        for k in (2, 1, 0):
            a, b = k * T, (k + 1) * T
            right[a:b, :] = w[a:b, lead:] - dot32(w[a:b, b:lead], right[b:, :])
        self.piv[...] = w[lead:, lead:joint]
        res = w[lead:, joint:]
        logs = negative_inverse(self.piv)
        sinv = -self.piv[...]
        u = dot32(sinv, res)
        quad = jnp.sum(res * u, axis=0, keepdims=True)
        inner = sinv - u * jnp.transpose(u)
        lane = lax.broadcasted_iota(jnp.int32, (T, T), 1)
        for k in range(5):
            rs = slice(k * T, (k + 1) * T)
            e = -right[rs, :T] if k < 4 else jnp.where(diagonal(), 1.0, 0.0)
            alpha = right[rs, T:] if k < 4 else jnp.zeros((T, T), jnp.float32)
            v = dot32(e, u)
            left = (-dot32(e, inner), jnp.where(lane == 0, alpha, jnp.where(lane == 1, v, 0.0)))
            for i, term in enumerate(left + (e, jnp.where(lane == 0, v, jnp.where(lane == 1, alpha, 0.0)))):
                cols = slice(i % 2 * T, (i % 2 + 1) * T)
                self.ext[i // 2 * 2, rs, cols], self.ext[i // 2 * 2 + 1, rs, cols] = split(term)
        return -0.5 * (quad + logs) - 0.5 * T * math.log(2.0 * math.pi)

    def grad_rows(self, k):
        rs = slice(k * T, (k + 1) * T)
        col = lax.broadcasted_iota(jnp.int32, (T, self.joint), 1)
        row = lax.broadcasted_iota(jnp.int32, (T, self.joint), 0)
        across = (((1,), (1,)), ((), ()))
        m = add_up(
            [
                lax.dot_general(self.ext[i, rs, :], self.ext[j], across, preferred_element_type=jnp.float32)
                for i, j in ((0, 3), (1, 2), (0, 2))
            ]
        )
        sym = jnp.where(col == row + k * T, 0.0, m * self.kern[rs, :] * (-0.5 / self.width)).astype(jnp.bfloat16)
        rowsum = jnp.sum(sym.astype(jnp.float32), axis=1, keepdims=True)
        part = jnp.dot(sym, self.x[...], preferred_element_type=jnp.float32)
        return 2.0 * (rowsum * self.x[rs, :].astype(jnp.float32) - part)


def diagonal():
    return lax.broadcasted_iota(jnp.int32, (T, T), 0) == lax.broadcasted_iota(jnp.int32, (T, T), 1)


def whole_kernel(cond_ref, feat_ref, obs_ref, value_ref, out_ref,
                 m0, m1, mz, mxy, own, row, obs0, obs1, obs2, oz, oy, ox,
                 near_mine, near_other, hot_mine, hot_other, slots, zgot, ygot, held, whole,
                 x, kern, work, piv, inverse, right, ext, squares,
                 back_mine, back_other, back_got, side_mine, side_other, side_got, near_out, near_got,
                 slots2, hot2, zgot2, xgot2, ygot2, held2,
                 msem, rsem, osem, nsem, psem, zsem, ysem, xsem, gsem, fsem,
                 nsem2, psem2, zsem2, xsem2, ysem2, gsem2):
    place = Place()
    terms = Terms(x, kern, work, piv, inverse, right, ext, squares)
    greeted = place.greet()
    ids = lax.broadcasted_iota(jnp.int32, (G, T), 0) * T + lax.broadcasted_iota(jnp.int32, (G, T), 1)
    marks = jnp.zeros((G, T), jnp.float32)
    for c in range(OWN):
        for k in (2, 3):
            marks = jnp.where(ids == cond_ref[c, k], 1.0, marks)
    m0[...] = marks
    obs_rows = obs_ref[...].astype(jnp.float32)
    for c in range(OWN):
        own[c, :T, :] = feat_ref[c * T : (c + 1) * T, :]
        own[c, T:, :] = jnp.broadcast_to(obs_rows[c : c + 1, :], (PACK - T, T)).astype(jnp.bfloat16)
    near_mine[:OWN] = own[...]
    for c in range(OWN):
        row[NX - 1, c * T : (c + 1) * T, :] = feat_ref[c * T : (c + 1) * T, :]
    place.meet(greeted)
    stage = start_stage(m0, mz, msem.at[:, pl.ds(0, NZ - 1)], place.along_z, NZ)
    rows = start_stage(feat_ref, row, rsem, place.along_x, NX)
    near = []
    for by in (1, 2):
        near.append(send(own, near_mine.at[pl.ds(by * OWN, OWN)], nsem, by - 1, place.along_blk(by)))
    early = [send(own, near_other.at[pl.ds(0, OWN)], psem, 0, place.partner())]
    m1[...] = end_stage(stage, m0[...], mz)
    stage = start_stage(m1, mxy, msem.at[:, pl.ds(NZ - 1, NX * NY - 1)], place.along_xy, NX * NY)
    for by in (1, 2):
        near[by - 1].wait()
        part = pl.ds(by * OWN, OWN)
        early.append(send(near_mine.at[part], near_other.at[part], psem, by, place.partner()))
    near_ids = []
    for s in range(OWN * (NEAR + 1)):
        near_ids.append((place.blk + NX * NZ * NY - s // OWN) % (NX * NZ * NY) * OWN + s % OWN)
    near_w = [[jnp.where(cond_ref[place.rep, k] == i, 1.0, 0.0) for i in near_ids] for k in range(2)]
    own_w = [jnp.where(place.rep == c, 1.0, 0.0) for c in range(OWN)]
    count = len(near_ids)
    early[0].wait()
    terms.place_rows(
        4,
        weighted(own_w, [near_mine[c] for c in range(OWN)]),
        weighted(own_w, [near_other[c] for c in range(OWN)]),
    )
    for copy in early[1:]:
        copy.wait()
    for k in range(2):
        terms.place_rows(
            k,
            weighted(near_w[k], [near_mine[s] for s in range(count)]),
            weighted(near_w[k], [near_other[s] for s in range(count)]),
        )
    terms.near_first()
    marks = end_stage(stage, m1[...], mxy)
    for copy in rows:
        copy.wait()
    quarter = pl.ds(place.x * (T // NX), T // NX)
    picks = pick_weights(place.blk * OWN, marks)
    row_picks = [picks]
    blocks = [row[NX - 1, pl.ds(c * T + place.x * (T // NX), T // NX), :] for c in range(OWN)]
    for o in range(1, NX):
        row_picks.append(pick_weights(place.along_x(NX - o)[0] * OWN, marks))
        blocks += [row[o - 1, pl.ds(c * T + place.x * (T // NX), T // NX), :] for c in range(OWN)]
    for s in range(HOT):
        slots[s] = weighted([p[s] for ps in row_picks for p in ps], blocks).astype(jnp.bfloat16)
    obs = jnp.zeros((HOT, T), jnp.float32)
    for s in range(HOT):
        line = weighted([p[s] for p in picks], [obs_rows[c : c + 1, :] for c in range(OWN)])
        obs = jnp.where(lax.broadcasted_iota(jnp.int32, (HOT, T), 0) == s, line, obs)
    obs0[...] = obs
    stage = start_scatter(place, slots, zgot, zsem)
    obs_stage = start_stage(obs0, oz, osem.at[:, pl.ds(0, NZ - 1)], place.along_z, NZ)
    named = jnp.where(marks > 0.5, 1.0, 0.0)
    hot_w = []
    for k in (2, 3):
        rank = jnp.sum(jnp.where(ids < cond_ref[place.rep, k], named, 0.0), keepdims=True)
        hot_w.append([jnp.where(jnp.abs(rank - s) < 0.5, 1.0, 0.0) for s in range(HOT)])
    negative_inverse(piv, half=True)
    held[0] = end_stage(stage, slots[place.z], zgot).astype(held.dtype)
    obs1[...] = end_stage(obs_stage, obs0[...], oz)
    stage = start_stage(held.at[0], ygot, ysem, place.along_y, NY)
    obs_stage = start_stage(obs1, oy, osem.at[:, pl.ds(NZ - 1, NY - 1)], place.along_y, NY)
    negative_inverse(piv, half=True)
    held[1] = end_stage(stage, held[0], ygot).astype(held.dtype)
    obs2[...] = end_stage(obs_stage, obs1[...], oy)
    whole[quarter, :] = held[1]
    stage = [send(held.at[1], whole.at[quarter], xsem, o - 1, place.along_x(o)) for o in range(1, NX)]
    obs_stage = start_stage(obs2, ox, osem.at[:, pl.ds(NZ + NY - 2, NX - 1)], place.along_x, NX)
    terms.near_update(0)
    for copy in stage:
        copy.wait()
    hot_obs = end_stage(obs_stage, obs2[...], ox)
    stage = start_gather(place, whole, hot_mine, gsem)
    passed = [send(whole, hot_other.at[place.z], fsem, 0, place.partner())]
    negative_inverse(piv)
    terms.near_update(1)
    for o in range(1, NZ):
        stage[o - 1].wait()
        slot = (place.z + NZ - o) % NZ
        passed.append(send(hot_mine.at[slot], hot_other.at[slot], fsem, o, place.partner()))
    mine = [weighted(w, [hot_mine[s] for s in range(HOT)]) for w in hot_w]
    lines = [weighted(w, [hot_obs[s : s + 1, :] for s in range(HOT)]) for w in hot_w]
    for copy in passed:
        copy.wait()
    for k in (0, 1):
        terms.place_rows(2 + k, mine[k], weighted(hot_w[k], [hot_other[s] for s in range(HOT)]), lines[k])
    value_ref[...] = terms.finish()
    grads = [terms.grad_rows(k) for k in (2, 3)]
    for s in range(HOT):
        total = weighted([w[s] for w in hot_w], grads).astype(jnp.bfloat16)
        back_mine[s] = total[:, :T]
        back_other[s] = total[:, T:]
    hot_copy = send(back_other, back_got, psem2, 0, place.partner())
    grads = [terms.grad_rows(0)]
    hot_copy.wait()
    slots2[...] = (back_mine[...].astype(jnp.float32) + back_got[...].astype(jnp.float32)).astype(jnp.bfloat16)
    stage = start_scatter(place, slots2, zgot2, zsem2)
    grads += [terms.grad_rows(k) for k in (1, 4)]
    for s in range(count):
        weights = [near_w[0][s], near_w[1][s]] + ([own_w[s]] if s < OWN else [])
        total = weighted(weights, grads).astype(jnp.bfloat16)
        side_mine[s] = total[:, :T]
        side_other[s] = total[:, T:]
    side_copy = send(side_other, side_got, psem2, 1, place.partner())
    side_copy.wait()
    part = pl.ds(OWN, OWN * NEAR)
    near_out[...] = (side_mine[part].astype(jnp.float32) + side_got[part].astype(jnp.float32)).astype(jnp.bfloat16)
    near = []
    for by in (1, 2):
        part = pl.ds((by - 1) * OWN, OWN)
        near.append(send(near_out.at[part], near_got.at[part], nsem2, by - 1, place.along_blk(-by)))
    held2[0] = end_stage(stage, slots2[place.z], zgot2).astype(held2.dtype)
    stage = start_stage(held2.at[0], xgot2, xsem2, place.along_x, NX)
    held2[1] = end_stage(stage, held2[0], xgot2).astype(held2.dtype)
    stage = start_stage(held2.at[1], ygot2, ysem2, place.along_y, NY)
    held2[2] = end_stage(stage, held2[1], ygot2).astype(held2.dtype)
    stage = start_gather(place, held2.at[2], hot2, gsem2)
    for copy in near:
        copy.wait()
    for c in range(OWN):
        total = side_mine[c].astype(jnp.float32) + side_got[c].astype(jnp.float32)
        for by in range(NEAR):
            total = total + near_got[by * OWN + c].astype(jnp.float32)
        out_ref[c * T : (c + 1) * T, :] = total
    for copy in stage:
        copy.wait()
    for c in range(OWN):
        rs = slice(c * T, (c + 1) * T)
        out_ref[rs, :] = out_ref[rs, :] + weighted(picks[c], [hot2[s] for s in range(HOT)])


def half(*shape):
    return pltpu.VMEM(shape, jnp.bfloat16)


def full(*shape):
    return pltpu.VMEM(shape, jnp.float32)


def dma(count):
    return pltpu.SemaphoreType.DMA((2, count))


def body(features, observations, cond_ids):
    per_dev = cond_ids.shape[0]
    width = features.shape[1]
    joint = (cond_ids.shape[1] + 1) * T
    count = OWN * (NEAR + 1)
    ring = [NZ - 1, NX - 1, NY - 1]
    value, grad = pl.pallas_call(
        whole_kernel,
        out_shape=(
            jax.ShapeDtypeStruct((G, T), jnp.float32),
            jax.ShapeDtypeStruct((per_dev * T, width), jnp.float32),
        ),
        in_specs=[pl.BlockSpec(memory_space=pltpu.SMEM), VMEM, VMEM],
        out_specs=(VMEM, VMEM),
        scratch_shapes=[full(G, T)] * 2
        + [full(n, G, T) for n in (NZ - 1, NX * NY - 1)]
        + [half(OWN, PACK, T), half(NX, OWN * T, T)]
        + [full(HOT, T)] * 3
        + [full(n - 1, HOT, T) for n in (NZ, NY, NX)]
        + [half(count, PACK, T)] * 2
        + [half(HOT, T, T)] * 2
        + [half(n, T // NX, T) for n in (HOT, NZ - 1, NY - 1, 2)]
        + [half(T, T)]
        + [
            half(joint, 2 * T),
            full(joint, joint),
            full(joint, joint + T),
            full(T, T),
            full(2, T, T),
            full(joint - T, 2 * T),
            half(4, joint, 2 * T),
            full(joint, T),
        ]
        + [half(HOT, T, T)] * 3
        + [half(count, T, T)] * 3
        + [half(OWN * NEAR, T, T)] * 2
        + [half(HOT, T, T)] * 2
        + [half(n, T, T) for n in ring + [3]]
        + [dma(n) for n in (NZ + NX * NY - 2, NX - 1, sum(ring), NEAR, NEAR + 1)]
        + [dma(n) for n in (NZ - 1, NY - 1, NX - 1, NZ - 1, NZ)]
        + [dma(n) for n in (NEAR, 2, *ring, NZ - 1)],
        compiler_params=pltpu.CompilerParams(
            collective_id=0, has_side_effects=True, vmem_limit_bytes=50 << 20
        ),
        name="block_vecchia",
    )(cond_ids, features, observations)
    return (value[0, :1], grad)


def solution(mesh):
    placed = (P("blk", "rep"), P("blk", None), P("blk", None))
    return jax.shard_map(
        body,
        mesh=mesh,
        in_specs=placed,
        out_specs=(P(("blk", "rep")), P("blk", "rep")),
        check_vma=False,
    )
```
